32 devices in a mesh: snap: 2 (over x), gx: 16 (over z, y, core).
Axes of the slice: x: 2, y: 2, z: 4, core: 2. Of those that a mesh axis runs over, the one named last changes fastest.
Arguments:
- component_shares: float32 [22, 160, 32, 128], P(None, ('snap', 'gx')), parts along dimension 1, may hold values from 0.01 to 1
- thermal_ratio: float32 [160, 32, 128], P(('snap', 'gx')), parts along dimension 0, may hold values from 0.5 to 2.5
- fuel_share: float32 [160, 32, 128], P(('snap', 'gx')), parts along dimension 0, may hold values from 0 to 1
- species_mass_unit: float32 [22], replicated, may hold values from 0.5 to 2
- formation_energy: float32 [22], replicated, may hold values from -4 to 4
- frequency_factor: float32 [206], replicated, may hold values from 0.5 to 2
- arrhenius_barrier: float32 [206], replicated, may hold values from 0.5 to 4
- product_minus_reactant: int32 [206, 22], replicated, may hold values from -1 to 2, as said below
- particle_voxel_position: int32 [32, 16, 64], P(('snap', 'gx')), parts along dimension 0, may hold values from 0 to 20479, as said below
- particle_voxel_offset: float32 [32, 16, 3, 64], P(('snap', 'gx')), parts along dimension 0, may hold values from 0 to 1
- particle_active_total: int32 [32, 16], P(('snap', 'gx')), parts along dimension 0, may hold values from 0 to 64, as said below
Outputs:
- samples: float32 [32, 16, 4, 64], P(('snap', 'gx')), parts along dimension 0
The draws below stay inside these ranges and needn't reach their ends.
There are 2 independent parts, one for each index of `snap`. The reference program is written for one: setup_inputs(seed, part) draws one part's arguments, and reference() takes and returns one part's arrays. A program takes and returns all parts, laid end to end along the dimension named above; an argument that names none is the same for every part. Nothing has to cross between parts.
Inputs may be any that keep to these rules, and one draw needn't show every extreme that they name: `product_minus_reactant`: each row has two reactants of coefficient -1 and two products of coefficient 1 or 2, at four different species. `particle_voxel_position`: every slot, live or not, names a cell of its owner brick, flattened as (plane * 32 + y) * 128 + z with plane below 5. `particle_active_total`: at most 64; in every draw some owner brick receives 64 live tracers from every source device.
All inputs are finite; a program needn't handle non-finite values.
Results may differ from the reference program's by a relative error of at most 0.000068.
Values sent between devices are 32-bit elements; how exact they have to be, the bound alone decides.
A program may use at most 64 MiB of HBM per device.

```python
import math
import jax
import jax.numpy as jnp
from jax import lax

SPECIES = 22
REACTIONS = 206
CX = 5
SPAN_BINS_FIRST = 32
SPAN_BINS_SECOND = 128
CAP = 64
BRICKS = 16
AXIAL_SLICES = 80


def draw_product_minus_reactant(key, part):
    row_keys = jax.random.split(jax.random.fold_in(key, 37), REACTIONS)
    chosen = jax.vmap(lambda single: jax.random.permutation(single, SPECIES))(row_keys)
    coeffs = jax.random.randint(jax.random.fold_in(key, 41), (REACTIONS, 2), 1, 3)
    labels = jnp.arange(SPECIES, dtype=jnp.int32)[None, :]
    netto = -(chosen[:, 0:1] == labels).astype(jnp.int32) - (chosen[:, 1:2] == labels).astype(jnp.int32)
    netto = netto + coeffs[:, 0:1] * (chosen[:, 2:3] == labels).astype(jnp.int32)
    netto = netto + coeffs[:, 1:2] * (chosen[:, 3:4] == labels).astype(jnp.int32)
    return netto.astype(jnp.int32)


def draw_particle_voxel_position(key, part):
    key_x, key_y, key_z = jax.random.split(jax.random.fold_in(key, 23), 3)
    layout = (BRICKS, BRICKS, CAP)
    plane = jax.random.randint(key_x, layout, 0, CX)
    row_y = jax.random.randint(key_y, layout, 0, SPAN_BINS_FIRST)
    row_z = jax.random.randint(key_z, layout, 0, SPAN_BINS_SECOND)
    return ((plane * SPAN_BINS_FIRST + row_y) * SPAN_BINS_SECOND + row_z).astype(jnp.int32)


def draw_particle_active_total(key, part):
    key_level, key_count, key_full = jax.random.split(jax.random.fold_in(key, 11), 3)
    level = jax.random.randint(key_level, (BRICKS,), 3, 6)
    raw_count = jax.random.randint(key_count, (BRICKS, BRICKS), 0, 1 << 20)
    counts = CAP * level[None, :] // 4 - raw_count % (CAP * level[None, :] // 8 + 1)
    counts = jnp.clip(counts, 0, CAP)
    filled = jax.random.randint(key_full, (), 0, BRICKS)
    counts = jnp.where(jnp.arange(BRICKS, dtype=jnp.int32)[None, :] == filled, CAP, counts)
    return counts.astype(jnp.int32)


def level_of(own_key, extent, pieces, smallest, largest):
    factor_of = 1.0
    for axis_at, parts in pieces:
        steps = jax.random.uniform(jax.random.fold_in(jax.random.fold_in(own_key, 6), axis_at), (parts,), jnp.float32, smallest / len(pieces), largest / len(pieces))
        factor_of = factor_of * jnp.repeat(jnp.exp(steps), extent[axis_at] // parts).reshape((-1,) + (1,) * (len(extent) - 1 - axis_at))
    return factor_of


def gaussian(own_key, shape, deviation, bound, kind=jnp.bfloat16):
    array = deviation * jax.random.normal(own_key, shape, jnp.float32)
    return jnp.clip(array, min=-bound, max=bound).astype(kind)


def setup_inputs(seed: int = 0, part: int = 0) -> dict:
    streams_of = jax.random.split(jax.random.key(seed), 12)
    own_keys = jax.random.split(jax.random.fold_in(streams_of[11], part), 12)
    component_shares = jnp.clip(jnp.exp(math.log(1.0) - 4.6051702 * jax.random.uniform(own_keys[0], (SPECIES, AXIAL_SLICES, SPAN_BINS_FIRST, SPAN_BINS_SECOND), jnp.float32) ** level_of(own_keys[0], (SPECIES, AXIAL_SLICES, SPAN_BINS_FIRST, SPAN_BINS_SECOND), ((1, 16),), -0.2, 0.2)), 0.01, 1.0)
    thermal_ratio = jnp.clip(0.5 + 2.0 * jax.random.uniform(own_keys[1], (AXIAL_SLICES, SPAN_BINS_FIRST, SPAN_BINS_SECOND), jnp.float32) ** level_of(own_keys[1], (AXIAL_SLICES, SPAN_BINS_FIRST, SPAN_BINS_SECOND), ((0, 16),), -0.2, 0.2), 0.5, 2.5)
    fuel_share = jnp.clip(1.0 * jax.random.uniform(own_keys[2], (AXIAL_SLICES, SPAN_BINS_FIRST, SPAN_BINS_SECOND), jnp.float32) ** level_of(own_keys[2], (AXIAL_SLICES, SPAN_BINS_FIRST, SPAN_BINS_SECOND), ((0, 16),), -0.2, 0.2), 0.0, 1.0)
    species_mass_unit = jnp.clip(jnp.exp(jax.random.uniform(streams_of[3], (SPECIES,), jnp.float32, math.log(0.5), math.log(2.0))), 0.5, 2.0)
    formation_energy = gaussian(streams_of[4], (SPECIES,), 1.0, 4.0, jnp.float32)
    frequency_factor = jnp.clip(jnp.exp(jax.random.uniform(streams_of[5], (REACTIONS,), jnp.float32, math.log(0.5), math.log(2.0))), 0.5, 2.0)
    arrhenius_barrier = jnp.clip(jnp.exp(jax.random.uniform(streams_of[6], (REACTIONS,), jnp.float32, math.log(0.5), math.log(4.0))), 0.5, 4.0)
    product_minus_reactant = draw_product_minus_reactant(jax.random.fold_in(streams_of[11], 71), part)
    particle_voxel_position = draw_particle_voxel_position(jax.random.fold_in(jax.random.fold_in(streams_of[11], part), 71), part)
    particle_voxel_offset = jnp.clip(1.0 * jax.random.uniform(own_keys[9], (BRICKS, BRICKS, 3, CAP), jnp.float32) ** level_of(own_keys[9], (BRICKS, BRICKS, 3, CAP), ((0, 16),), -0.2, 0.2), 0.0, 1.0)
    particle_active_total = draw_particle_active_total(jax.random.fold_in(jax.random.fold_in(streams_of[11], part), 71), part)
    return {"component_shares": component_shares, "thermal_ratio": thermal_ratio, "fuel_share": fuel_share, "species_mass_unit": species_mass_unit, "formation_energy": formation_energy, "frequency_factor": frequency_factor, "arrhenius_barrier": arrhenius_barrier, "product_minus_reactant": product_minus_reactant, "particle_voxel_position": particle_voxel_position, "particle_voxel_offset": particle_voxel_offset, "particle_active_total": particle_active_total}


stencil_coeffs = (0.8, -0.2, 4.0 / 105.0, -1.0 / 280.0)
highest_precision = lax.Precision.HIGHEST


def heat_block(species_block, temper, kinetic_exponents, combined_thermal_output, log_rate_prefactor, arrhenius_barrier, log_molar_weight):
    log_conc = jnp.log(species_block) - log_molar_weight[:, None] - jnp.log(temper)[None, :]
    log_rate = jnp.dot(kinetic_exponents, log_conc, precision=highest_precision, preferred_element_type=jnp.float32)
    log_rate = log_rate + log_rate_prefactor[:, None] - arrhenius_barrier[:, None] / temper[None, :]
    return -jnp.dot(combined_thermal_output, jnp.exp(log_rate), precision=highest_precision, preferred_element_type=jnp.float32)


def thermal_output_grid(species_flat, temper_flat, kinetic_exponents, combined_thermal_output, log_rate_prefactor, arrhenius_barrier, log_molar_weight):
    cells = temper_flat.shape[0]
    block_len = math.gcd(cells, 8192)
    blocks = cells // block_len

    def one_block(index):
        start = index * block_len
        return heat_block(lax.dynamic_slice_in_dim(species_flat, start, block_len, 1),
                          lax.dynamic_slice_in_dim(temper_flat, start, block_len, 0),
                          kinetic_exponents, combined_thermal_output, log_rate_prefactor, arrhenius_barrier, log_molar_weight)

    return lax.map(one_block, jnp.arange(blocks, dtype=jnp.int32)).reshape(cells)


def gradient(field, axis):
    total = jnp.zeros_like(field)
    for offset in range(1, 5):
        coeff = stencil_coeffs[offset - 1]
        total = total + coeff * (jnp.roll(field, -offset, axis) - jnp.roll(field, offset, axis))
    return total


def reference(component_shares, thermal_ratio, fuel_share, species_mass_unit, formation_energy, frequency_factor, arrhenius_barrier, product_minus_reactant, particle_voxel_position, particle_voxel_offset, particle_active_total):
    kinetic_exponents = jnp.maximum(-product_minus_reactant, 0).astype(jnp.float32)
    combined_thermal_output = jnp.dot(product_minus_reactant.astype(jnp.float32), formation_energy, precision=highest_precision, preferred_element_type=jnp.float32)
    thermal_output = thermal_output_grid(component_shares.reshape(component_shares.shape[0], -1), thermal_ratio.reshape(-1), kinetic_exponents, combined_thermal_output,
                      jnp.log(frequency_factor), arrhenius_barrier, jnp.log(species_mass_unit)).reshape(thermal_ratio.shape)
    grad_x = gradient(fuel_share, 0)
    grad_y = gradient(fuel_share, 1)
    grad_z = gradient(fuel_share, 2)
    smoothed_quantity = 0.5 * jnp.power(thermal_ratio, 0.7)
    gradient_squared_mixing = 2.0 * smoothed_quantity * (grad_x * grad_x + grad_y * grad_y + grad_z * grad_z)
    quantity_pile = jnp.stack([thermal_ratio, fuel_share, gradient_squared_mixing, thermal_output]).reshape(4, -1)
    owner = jnp.arange(BRICKS, dtype=jnp.int32)[None, :, None]
    cell_x = owner * CX + particle_voxel_position // (SPAN_BINS_FIRST * SPAN_BINS_SECOND)
    cell_y = (particle_voxel_position // SPAN_BINS_SECOND) % SPAN_BINS_FIRST
    cell_z = particle_voxel_position % SPAN_BINS_SECOND
    frac_x = particle_voxel_offset[:, :, 0, :]
    frac_y = particle_voxel_offset[:, :, 1, :]
    frac_z = particle_voxel_offset[:, :, 2, :]
    total = jnp.zeros((4, BRICKS, BRICKS, CAP), jnp.float32)
    for step_x in (0, 1):
        for step_y in (0, 1):
            for step_z in (0, 1):
                corner = (((cell_x + step_x) % AXIAL_SLICES) * SPAN_BINS_FIRST + (cell_y + step_y) % SPAN_BINS_FIRST) * SPAN_BINS_SECOND + (cell_z + step_z) % SPAN_BINS_SECOND
                weight = (frac_x if step_x else 1.0 - frac_x) * (frac_y if step_y else 1.0 - frac_y) * (frac_z if step_z else 1.0 - frac_z)
                total = total + weight[None] * quantity_pile[:, corner.astype(jnp.int32)]
    sampled = jnp.moveaxis(total, 0, 2)
    live_slot = jnp.arange(CAP, dtype=jnp.int32)[None, None, :] < particle_active_total[:, :, None]
    return jnp.where(live_slot[:, :, None, :], sampled, jnp.float32(0.0))
```

```python
import functools

import jax
import jax.numpy as jnp
from jax import lax
from jax.experimental import pallas as pl
from jax.experimental.pallas import tpu as pltpu
from jax.sharding import PartitionSpec as P

stencil_coeffs = (0.8, -0.2, 4.0 / 105.0, -1.0 / 280.0)
reach = 4
log2e = 1.4426950408889634
MESH = pl.DeviceIdType.MESH
f32 = jnp.float32
bf16 = jnp.bfloat16


def split3(x):
    hi = x.astype(bf16)
    rest = x - hi.astype(f32)
    mid = rest.astype(bf16)
    lo = (rest - mid.astype(f32)).astype(bf16)
    return hi, mid, lo


def split2(x):
    hi = x.astype(bf16)
    return hi, (x - hi.astype(f32)).astype(bf16)


def kernel(
    n,
    species_hbm,
    t_ref,
    fuel_ref,
    par_ref,
    stoich_ref,
    pos_ref,
    off_ref,
    out_ref,
    species,
    feat,
    weights,
    heat_weight,
    heat,
    fcat,
    halo_before,
    halo_after,
    edge_t,
    edge_out,
    edge_in,
    pack,
    recv,
    back,
    home,
    load_sem,
    halo_send,
    halo_recv,
    out_send,
    out_recv,
    home_send,
    home_recv,
):
    me = lax.axis_index("gx")
    nxt, prv = lax.rem(me + 1, n), lax.rem(me + n - 1, n)
    n_species, planes, ny, nz = species_hbm.shape
    slots = pos_ref.shape[1]
    reactions = stoich_ref.shape[0]
    padded = weights.shape[0]
    group = 32

    loads = [
        pltpu.make_async_copy(species_hbm.at[:, p], species.at[p], load_sem.at[p])
        for p in range(planes)
    ]
    for copy in loads:
        copy.start()

    barrier = pltpu.get_barrier_semaphore()

    def greet(k, _):
        pl.semaphore_signal(
            barrier, inc=1, device_id={"gx": lax.rem(me + k, n)}, device_id_type=MESH
        )
        return 0

    lax.fori_loop(1, n, greet, 0)

    def pack_one(d, _):
        pack[d, 0:1, 0:slots] = pos_ref[pl.ds(d, 1), :].astype(f32)
        pack[d, 1:4, 0:slots] = off_ref[d]
        return 0

    lax.fori_loop(0, n, pack_one, 0)

    lane = lax.broadcasted_iota(jnp.int32, (padded, 128), 1)
    stoich = jnp.zeros((padded, 128), f32)
    weights_f = jnp.zeros((padded, 128), f32)
    heat_weight[...] = jnp.zeros_like(heat_weight)
    feat_rows = jnp.zeros((ny, nz), f32)
    stoich_pad = heat_weight
    stoich_pad[0:reactions, 0:n_species] = stoich_ref[...].astype(f32)
    stoich = stoich_pad[...]
    orders = jnp.maximum(-stoich, 0.0)
    par = par_ref[...]
    net = -jnp.sum(stoich * par[3:4, 0:128], axis=1, keepdims=True)
    mass_term = jnp.sum(orders * jnp.log(par[2:3, 0:128]), axis=1, keepdims=True)
    columns = jnp.transpose(
        jnp.concatenate([jnp.log(par[0:1]), par[1:2], jnp.zeros((126, 256), f32)], axis=0)
    )[0:padded]
    offset = (columns[:, 0:1] - mass_term) * log2e
    barrier_col = columns[:, 1:2] * (-log2e)
    in_group = lane % group
    live_lane = lane < 3 * group
    weights_f = orders + pltpu.roll(orders, group, 1) + pltpu.roll(orders, 2 * group, 1)
    for j, part in enumerate(split3(barrier_col)):
        weights_f = jnp.where(in_group == n_species + j, part.astype(f32), weights_f)
    for j, part in enumerate(split3(offset)):
        weights_f = jnp.where(in_group == n_species + 3 + j, part.astype(f32), weights_f)
    weights[...] = jnp.where(live_lane, weights_f, 0.0).astype(bf16)
    heat_weight[...] = jnp.broadcast_to(net, heat_weight.shape)

    ones = jnp.ones((ny, nz), f32)
    for j in range(3):
        feat[(n_species + 3 + j) * ny : (n_species + 4 + j) * ny, :] = ones
    for j in range(n_species + 6, group):
        feat[j * ny : (j + 1) * ny, :] = jnp.zeros((ny, nz), f32)

    batch = 8

    def heat_plane(p):
        loads[p].wait()
        temper = t_ref[p]
        log_t = jnp.log(temper)
        for s in range(n_species):
            feat[s * ny : (s + 1) * ny, :] = (jnp.log(species[p, s]) - log_t) * log2e
        inverse = 1.0 / temper
        for j in range(3):
            feat[(n_species + j) * ny : (n_species + j + 1) * ny, :] = inverse

        def rows(i, _):
            for b in range(0, batch, 2):
                r = i * batch + b
                f = jnp.concatenate(
                    [
                        feat[pl.ds(r, group, stride=ny), :],
                        feat[pl.ds(r + 1, group, stride=ny), :],
                    ],
                    axis=1,
                )
                x = jnp.dot(
                    weights[:, 0 : 3 * group],
                    jnp.concatenate(split3(f), axis=0),
                    preferred_element_type=f32,
                )
                rate = jnp.exp2(x)
                hw = heat_weight[...]
                for h in range(2):
                    term = rate[:, h * 128 : (h + 1) * 128] * hw
                    total = jnp.sum(term.reshape(padded // 8, 8, 128), axis=0)
                    heat[pl.ds(p * ny + r + h, 1), :] = jnp.sum(total, axis=0, keepdims=True)
            return 0

        lax.fori_loop(0, ny // batch, rows, 0)

    def put(p, f, value):
        hi, lo = split2(value)
        r = (p * 4 + f) * ny
        fcat[r : r + ny, 0:nz] = hi
        fcat[r : r + ny, nz : 2 * nz] = lo

    def plane_of(q):
        if q < 0:
            return halo_before[q + reach]
        if q >= planes:
            return halo_after[q - planes]
        return fuel_ref[q]

    def dissip(p):
        centre = plane_of(p)
        gx = jnp.zeros_like(centre)
        gy = jnp.zeros_like(centre)
        gz = jnp.zeros_like(centre)
        for k in range(1, reach + 1):
            c = stencil_coeffs[k - 1]
            gx = gx + c * (plane_of(p + k) - plane_of(p - k))
            gy = gy + c * (pltpu.roll(centre, ny - k, 0) - pltpu.roll(centre, k, 0))
            gz = gz + c * (pltpu.roll(centre, nz - k, 1) - pltpu.roll(centre, k, 1))
        return jnp.exp(0.7 * jnp.log(t_ref[p])) * (gx * gx + gy * gy + gz * gz)

    def remote(src, dst, send, got, to):
        return pltpu.make_async_remote_copy(
            src_ref=src,
            dst_ref=dst,
            send_sem=send,
            recv_sem=got,
            device_id={"gx": to},
            device_id_type=MESH,
        )

    heat_plane(0)

    pl.semaphore_wait(barrier, n - 1)
    up = remote(
        fuel_ref.at[pl.ds(planes - reach, reach)], halo_before, halo_send.at[0], halo_recv.at[0], nxt
    )
    down = remote(fuel_ref.at[pl.ds(0, reach)], halo_after, halo_send.at[1], halo_recv.at[1], prv)
    down_t = remote(t_ref.at[0], edge_t, halo_send.at[2], halo_recv.at[2], prv)
    down_e = remote(edge_out, edge_in, halo_send.at[3], halo_recv.at[3], prv)
    up.start()

    def send_out(k, _):
        d = lax.rem(me + k, n)
        remote(pack.at[d], recv.at[me], out_send.at[d], out_recv.at[me], d).start()
        return 0

    lax.fori_loop(1, n, send_out, 0)
    down.start()
    down_t.start()
    recv[me] = pack[me]

    heat_plane(1)
    up.wait_recv()
    first = dissip(0)
    edge_out[0] = first
    edge_out[1] = heat[0:ny, :]
    for p in range(2, planes):
        heat_plane(p)
        if p == 2:
            down_e.start()
    down.wait_recv()
    for p in range(planes):
        put(p, 0, t_ref[p])
        put(p, 1, fuel_ref[p])
        put(p, 2, first if p == 0 else dissip(p))
        put(p, 3, heat[p * ny : (p + 1) * ny, :])
    down_t.wait_recv()
    down_e.wait_recv()
    put(planes, 0, edge_t[...])
    put(planes, 1, halo_after[0])
    put(planes, 2, edge_in[0])
    put(planes, 3, edge_in[1])

    def got_one(k, _):
        d = lax.rem(me + k, n)
        remote(pack.at[d], recv.at[d], out_send.at[d], out_recv.at[d], d).wait()
        return 0

    lax.fori_loop(1, n, got_one, 0)

    low = lax.broadcasted_iota(jnp.int32, (4, 128), 1) < slots
    z_label = lax.broadcasted_iota(jnp.int32, (nz, 256), 0).astype(f32)
    y_label = lax.broadcasted_iota(jnp.int32, (ny, 256), 0).astype(f32)

    def sample(g, _):
        halves = [
            jnp.where(low, recv[4 * g + 2 * h], pltpu.roll(recv[4 * g + 2 * h + 1], slots, 1))
            for h in range(2)
        ]
        t = jnp.concatenate(halves, axis=1)
        cell, fx, fy, fz = (t[i : i + 1] for i in range(4))
        cx = jnp.floor((cell + 0.5) * (1.0 / (ny * nz)))
        cell = cell - cx * (ny * nz)
        cy = jnp.floor((cell + 0.5) * (1.0 / nz))
        cz = cell - cy * nz
        cy1 = jnp.where(cy + 1.0 >= ny, 0.0, cy + 1.0)
        cz1 = jnp.where(cz + 1.0 >= nz, 0.0, cz + 1.0)
        wz = jnp.where(z_label == cz, 1.0 - fz, jnp.where(z_label == cz1, fz, 0.0))
        wy = jnp.where(y_label == cy, 1.0 - fy, jnp.where(y_label == cy1, fy, 0.0))
        wh, wl = split2(wz)
        both = jnp.concatenate([wh, wh], axis=0)
        acc = jnp.zeros((4, 8, 256), f32)
        for p in range(planes + 1):
            rows = slice(p * 4 * ny, (p + 1) * 4 * ny)
            a = jnp.dot(fcat[rows, :], both, preferred_element_type=f32)
            a = a + jnp.dot(fcat[rows, 0:nz], wl, preferred_element_type=f32)
            wx = jnp.where(cx == p, 1.0 - fx, jnp.where(cx == p - 1.0, fx, 0.0))
            a = a.reshape(4, ny // 8, 8, 256) * wy.reshape(ny // 8, 8, 256)[None]
            acc = acc + jnp.sum(a, axis=1) * wx.reshape(1, 1, 256)
        v = jnp.sum(acc, axis=1)
        for j in range(4):
            s = 4 * g + j
            block = v[:, (j // 2) * 128 : (j // 2 + 1) * 128]
            if j % 2:
                block = pltpu.roll(block, 128 - slots, 1)
            back[s] = block

            @pl.when(s != me)
            def _():
                remote(back.at[s], home.at[me], home_send.at[s], home_recv.at[me], s).start()

        return 0

    lax.fori_loop(0, n // 4, sample, 0)
    home[me] = back[me]

    def home_one(k, _):
        d = lax.rem(me + k, n)
        remote(back.at[d], home.at[d], home_send.at[d], home_recv.at[d], d).wait()
        return 0

    lax.fori_loop(1, n, home_one, 0)
    for copy in (up, down, down_t, down_e):
        copy.wait_send()
    out_ref[...] = home[...]


def local(
    component_shares,
    thermal_ratio,
    fuel_share,
    species_mass_unit,
    formation_energy,
    frequency_factor,
    arrhenius_barrier,
    product_minus_reactant,
    particle_voxel_position,
    particle_voxel_offset,
    particle_active_total,
):
    n = lax.axis_size("gx")
    n_species, planes, ny, nz = component_shares.shape
    reactions = frequency_factor.shape[0]
    slots = particle_voxel_position.shape[2]
    padded = (reactions + 7) // 8 * 8
    fill = lambda a, v: jnp.pad(a, (0, 256 - a.shape[0]), constant_values=v)
    par = jnp.stack(
        [
            fill(frequency_factor, 1.0),
            fill(arrhenius_barrier, 0.0),
            fill(species_mass_unit, 1.0),
            fill(formation_energy, 0.0),
        ]
    )
    vmem = pl.BlockSpec(memory_space=pltpu.VMEM)
    dma = pltpu.SemaphoreType.DMA
    returned = pl.pallas_call(
        functools.partial(kernel, n),
        out_shape=jax.ShapeDtypeStruct((n, 4, 128), f32),
        in_specs=[pl.BlockSpec(memory_space=pl.ANY)] + [vmem] * 6,
        out_specs=vmem,
        scratch_shapes=[
            pltpu.VMEM((planes, n_species, ny, nz), f32),
            pltpu.VMEM((32 * ny, nz), f32),
            pltpu.VMEM((padded, 128), bf16),
            pltpu.VMEM((padded, 128), f32),
            pltpu.VMEM((planes * ny, nz), f32),
            pltpu.VMEM(((planes + 1) * 4 * ny, 2 * nz), bf16),
            pltpu.VMEM((reach, ny, nz), f32),
            pltpu.VMEM((reach, ny, nz), f32),
            pltpu.VMEM((ny, nz), f32),
            pltpu.VMEM((2, ny, nz), f32),
            pltpu.VMEM((2, ny, nz), f32),
            pltpu.VMEM((n, 4, 128), f32),
            pltpu.VMEM((n, 4, 128), f32),
            pltpu.VMEM((n, 4, 128), f32),
            pltpu.VMEM((n, 4, 128), f32),
            dma((planes,)),
            dma((4,)),
            dma((4,)),
            dma((n,)),
            dma((n,)),
            dma((n,)),
            dma((n,)),
        ],
        compiler_params=pltpu.CompilerParams(collective_id=0, has_side_effects=True),
    )(
        component_shares,
        thermal_ratio,
        fuel_share,
        par,
        product_minus_reactant,
        particle_voxel_position[0],
        particle_voxel_offset[0],
    )
    live_slot = jnp.arange(slots, dtype=jnp.int32)[None, :] < particle_active_total[0][:, None]
    return jnp.where(live_slot[:, None, :], returned[:, :, 0:slots], f32(0.0))[None]


def solution(mesh):
    placed = (
        P(None, ("snap", "gx"), None, None),
        P(("snap", "gx"), None, None),
        P(("snap", "gx"), None, None),
        P(),
        P(),
        P(),
        P(),
        P(),
        P(("snap", "gx"), None, None),
        P(("snap", "gx"), None, None, None),
        P(("snap", "gx"), None),
    )
    return jax.shard_map(
        local,
        mesh=mesh,
        in_specs=placed,
        out_specs=P(("snap", "gx"), None, None, None),
        check_vma=False,
    )
```

```python
import functools

import jax
import jax.numpy as jnp
from jax import lax
from jax.experimental import pallas as pl
from jax.experimental.pallas import tpu as pltpu
from jax.sharding import PartitionSpec as P

stencil_coeffs = (0.8, -0.2, 4.0 / 105.0, -1.0 / 280.0)
reach = 4
log2e = 1.4426950408889634
MESH = pl.DeviceIdType.MESH
f32 = jnp.float32
bf16 = jnp.bfloat16


def split3(x):
    hi = x.astype(bf16)
    rest = x - hi.astype(f32)
    mid = rest.astype(bf16)
    lo = (rest - mid.astype(f32)).astype(bf16)
    return hi, mid, lo


def split2(x):
    hi = x.astype(bf16)
    return hi, (x - hi.astype(f32)).astype(bf16)


def kernel(
    n,
    species_hbm,
    t_ref,
    fuel_ref,
    mass_ref,
    formation_ref,
    frequency_ref,
    barrier_ref,
    stoich_ref,
    pos_ref,
    off_ref,
    live_ref,
    out_ref,
    species,
    feat,
    weights,
    heat_weight,
    table,
    heat,
    fcat,
    halo_before,
    halo_after,
    edge_t,
    edge_out,
    edge_in,
    pack,
    recv,
    back,
    home,
    load_sem,
    halo_send,
    halo_recv,
    out_send,
    out_recv,
    home_send,
    home_recv,
):
    me = lax.axis_index("gx")
    nxt, prv = lax.rem(me + 1, n), lax.rem(me + n - 1, n)
    n_species, planes, ny, nz = species_hbm.shape
    slots = pos_ref.shape[1]
    reactions = stoich_ref.shape[1]
    padded = weights.shape[0]
    group = 32

    loads = [
        pltpu.make_async_copy(species_hbm.at[:, p], species.at[p], load_sem.at[p])
        for p in range(planes)
    ]
    for copy in loads:
        copy.start()

    barrier = pltpu.get_barrier_semaphore()

    def greet(k, _):
        pl.semaphore_signal(
            barrier, inc=1, device_id={"gx": lax.rem(me + k, n)}, device_id_type=MESH
        )
        return 0

    lax.fori_loop(1, n, greet, 0)

    def pack_one(d, _):
        pack[d, 0:1, 0:slots] = pos_ref[pl.ds(d, 1), :].astype(f32)
        for i in range(3):
            pack[d, i + 1 : i + 2, 0:slots] = off_ref[i, pl.ds(d, 1), :]
        return 0

    lax.fori_loop(0, n, pack_one, 0)

    table[...] = jnp.zeros_like(table)
    stoich = stoich_ref[...].astype(f32)
    orders = jnp.maximum(-stoich, 0.0)
    same = lax.broadcasted_iota(jnp.int32, (n_species, n_species), 0) == lax.broadcasted_iota(
        jnp.int32, (n_species, n_species), 1
    )
    log_mass = jnp.sum(jnp.where(same, jnp.log(mass_ref[...]), 0.0), axis=1, keepdims=True)
    formation = jnp.sum(jnp.where(same, formation_ref[...], 0.0), axis=1, keepdims=True)
    net = -jnp.sum(stoich * formation, axis=0, keepdims=True)
    offset = jnp.log(frequency_ref[...]) - jnp.sum(orders * log_mass, axis=0, keepdims=True)
    extra = [
        part.astype(f32)
        for row in (barrier_ref[...] * (-log2e), offset * log2e)
        for part in split3(row)
    ]
    for j in range(3):
        table[j * group : j * group + n_species, 0:reactions] = orders
        for i, row in enumerate(extra):
            r = j * group + n_species + i
            table[r : r + 1, 0:reactions] = row
    table[3 * group : 3 * group + 1, 0:reactions] = net
    columns = jnp.transpose(table[...])[0:padded]
    weights[...] = columns.astype(bf16)
    heat_weight[...] = jnp.broadcast_to(columns[:, 3 * group : 3 * group + 1], (padded, 128))

    ones = jnp.ones((ny, nz), f32)
    for j in range(3):
        feat[(n_species + 3 + j) * ny : (n_species + 4 + j) * ny, :] = ones
    for j in range(n_species + 6, group):
        feat[j * ny : (j + 1) * ny, :] = jnp.zeros((ny, nz), f32)

    batch = 32

    def heat_plane(p):
        loads[p].wait()
        temper = t_ref[p]
        log_t = jnp.log(temper)
        for s in range(n_species):
            feat[s * ny : (s + 1) * ny, :] = (jnp.log(species[p, s]) - log_t) * log2e
        inverse = 1.0 / temper
        for j in range(3):
            feat[(n_species + j) * ny : (n_species + j + 1) * ny, :] = inverse

        def rows(i, _):
            for b in range(0, batch, 2):
                r = i * batch + b
                f = jnp.concatenate(
                    [
                        feat[pl.ds(r, group, stride=ny), :],
                        feat[pl.ds(r + 1, group, stride=ny), :],
                    ],
                    axis=1,
                )
                x = jnp.dot(
                    weights[:, 0 : 3 * group],
                    jnp.concatenate(split3(f), axis=0),
                    preferred_element_type=f32,
                )
                rate = jnp.exp2(x)
                hw = heat_weight[...]
                for h in range(2):
                    term = rate[:, h * 128 : (h + 1) * 128] * hw
                    total = jnp.sum(term.reshape(padded // 8, 8, 128), axis=0)
                    heat[pl.ds(p * ny + r + h, 1), :] = jnp.sum(total, axis=0, keepdims=True)
            return 0

        lax.fori_loop(0, ny // batch, rows, 0)

    def put(p, f, value):
        hi, lo = split2(value)
        r = (p * 4 + f) * ny
        fcat[r : r + ny, 0:nz] = hi
        fcat[r : r + ny, nz : 2 * nz] = lo

    def plane_of(q):
        if q < 0:
            return halo_before[q + reach]
        if q >= planes:
            return halo_after[q - planes]
        return fuel_ref[q]

    def dissip(p):
        centre = plane_of(p)
        gx = jnp.zeros_like(centre)
        gy = jnp.zeros_like(centre)
        gz = jnp.zeros_like(centre)
        for k in range(1, reach + 1):
            c = stencil_coeffs[k - 1]
            gx = gx + c * (plane_of(p + k) - plane_of(p - k))
            gy = gy + c * (pltpu.roll(centre, ny - k, 0) - pltpu.roll(centre, k, 0))
            gz = gz + c * (pltpu.roll(centre, nz - k, 1) - pltpu.roll(centre, k, 1))
        return jnp.exp(0.7 * jnp.log(t_ref[p])) * (gx * gx + gy * gy + gz * gz)

    def remote(src, dst, send, got, to):
        return pltpu.make_async_remote_copy(
            src_ref=src,
            dst_ref=dst,
            send_sem=send,
            recv_sem=got,
            device_id={"gx": to},
            device_id_type=MESH,
        )

    heat_plane(0)

    pl.semaphore_wait(barrier, n - 1)
    up = remote(
        fuel_ref.at[pl.ds(planes - reach, reach)], halo_before, halo_send.at[0], halo_recv.at[0], nxt
    )
    down = remote(fuel_ref.at[pl.ds(0, reach)], halo_after, halo_send.at[1], halo_recv.at[1], prv)
    down_t = remote(t_ref.at[0], edge_t, halo_send.at[2], halo_recv.at[2], prv)
    down_e = remote(edge_out, edge_in, halo_send.at[3], halo_recv.at[3], prv)
    up.start()

    def send_out(k, _):
        d = lax.rem(me + k, n)
        remote(pack.at[d], recv.at[me], out_send.at[d], out_recv.at[me], d).start()
        return 0

    lax.fori_loop(1, n, send_out, 0)
    down.start()
    down_t.start()
    recv[me] = pack[me]

    heat_plane(1)
    up.wait_recv()
    first = dissip(0)
    edge_out[0] = first
    edge_out[1] = heat[0:ny, :]
    for p in range(2, planes):
        heat_plane(p)
        if p == 2:
            down_e.start()
    down.wait_recv()
    for p in range(planes):
        put(p, 0, t_ref[p])
        put(p, 1, fuel_ref[p])
        put(p, 2, first if p == 0 else dissip(p))
        put(p, 3, heat[p * ny : (p + 1) * ny, :])
    down_t.wait_recv()
    down_e.wait_recv()
    put(planes, 0, edge_t[...])
    put(planes, 1, halo_after[0])
    put(planes, 2, edge_in[0])
    put(planes, 3, edge_in[1])

    def got_one(k, _):
        d = lax.rem(me + k, n)
        remote(pack.at[d], recv.at[d], out_send.at[d], out_recv.at[d], d).wait()
        return 0

    lax.fori_loop(1, n, got_one, 0)

    low = lax.broadcasted_iota(jnp.int32, (4, 128), 1) < slots
    z_label = lax.broadcasted_iota(jnp.int32, (nz, 256), 0).astype(f32)
    y_label = lax.broadcasted_iota(jnp.int32, (ny, 256), 0).astype(f32)

    def sample(step, _):
        g = lax.rem(me // 4 + 1 + step, n // 4)
        halves = [
            jnp.where(low, recv[4 * g + 2 * h], pltpu.roll(recv[4 * g + 2 * h + 1], slots, 1))
            for h in range(2)
        ]
        t = jnp.concatenate(halves, axis=1)
        cell, fx, fy, fz = (t[i : i + 1] for i in range(4))
        cx = jnp.floor((cell + 0.5) * (1.0 / (ny * nz)))
        cell = cell - cx * (ny * nz)
        cy = jnp.floor((cell + 0.5) * (1.0 / nz))
        cz = cell - cy * nz
        cy1 = jnp.where(cy + 1.0 >= ny, 0.0, cy + 1.0)
        cz1 = jnp.where(cz + 1.0 >= nz, 0.0, cz + 1.0)
        wz = jnp.where(z_label == cz, 1.0 - fz, jnp.where(z_label == cz1, fz, 0.0))
        wy = jnp.where(y_label == cy, 1.0 - fy, jnp.where(y_label == cy1, fy, 0.0))
        wh, wl = split2(wz)
        both = jnp.concatenate([wh, wh], axis=0)
        acc = jnp.zeros((4, 8, 256), f32)
        for p in range(planes + 1):
            rows = slice(p * 4 * ny, (p + 1) * 4 * ny)
            a = jnp.dot(fcat[rows, :], both, preferred_element_type=f32)
            a = a + jnp.dot(fcat[rows, 0:nz], wl, preferred_element_type=f32)
            wx = jnp.where(cx == p, 1.0 - fx, jnp.where(cx == p - 1.0, fx, 0.0))
            a = a.reshape(4, ny // 8, 8, 256) * wy.reshape(ny // 8, 8, 256)[None]
            acc = acc + jnp.sum(a, axis=1) * wx.reshape(1, 1, 256)
        v = jnp.sum(acc, axis=1)
        for j in range(4):
            s = 4 * g + j
            block = v[:, (j // 2) * 128 : (j // 2 + 1) * 128]
            if j % 2:
                block = pltpu.roll(block, 128 - slots, 1)
            back[s] = block

            @pl.when(s != me)
            def _():
                remote(back.at[s], home.at[me], home_send.at[s], home_recv.at[me], s).start()

        return 0

    lax.fori_loop(0, n // 4, sample, 0)
    home[me] = back[me]

    def home_one(k, _):
        d = lax.rem(me + k, n)
        remote(back.at[d], home.at[d], home_send.at[d], home_recv.at[d], d).wait()
        return 0

    lax.fori_loop(1, n, home_one, 0)
    for copy in (up, down, down_t, down_e):
        copy.wait_send()

    slot = lax.broadcasted_iota(jnp.int32, (4, slots), 1)

    def finish(d, _):
        out_ref[d] = jnp.where(slot < live_ref[0, d], home[d, :, 0:slots], 0.0)
        return 0

    lax.fori_loop(0, n, finish, 0)


def local(
    component_shares,
    thermal_ratio,
    fuel_share,
    species_mass_unit,
    formation_energy,
    frequency_factor,
    arrhenius_barrier,
    product_minus_reactant,
    particle_voxel_position,
    particle_voxel_offset,
    particle_active_total,
):
    n = lax.axis_size("gx")
    n_species, planes, ny, nz = component_shares.shape
    reactions = frequency_factor.shape[0]
    slots = particle_voxel_position.shape[2]
    padded = (reactions + 7) // 8 * 8
    vmem = pl.BlockSpec(memory_space=pltpu.VMEM)
    dma = pltpu.SemaphoreType.DMA
    samples = pl.pallas_call(
        functools.partial(kernel, n),
        out_shape=jax.ShapeDtypeStruct((n, 4, slots), f32),
        in_specs=[pl.BlockSpec(memory_space=pl.ANY)] + [vmem] * 9
        + [pl.BlockSpec(memory_space=pltpu.SMEM)],
        out_specs=vmem,
        scratch_shapes=[
            pltpu.VMEM((planes, n_species, ny, nz), f32),
            pltpu.VMEM((32 * ny, nz), f32),
            pltpu.VMEM((padded, 128), bf16),
            pltpu.VMEM((padded, 128), f32),
            pltpu.VMEM((128, (padded + 127) // 128 * 128), f32),
            pltpu.VMEM((planes * ny, nz), f32),
            pltpu.VMEM(((planes + 1) * 4 * ny, 2 * nz), bf16),
            pltpu.VMEM((reach, ny, nz), f32),
            pltpu.VMEM((reach, ny, nz), f32),
            pltpu.VMEM((ny, nz), f32),
            pltpu.VMEM((2, ny, nz), f32),
            pltpu.VMEM((2, ny, nz), f32),
            pltpu.VMEM((n, 4, 128), f32),
            pltpu.VMEM((n, 4, 128), f32),
            pltpu.VMEM((n, 4, 128), f32),
            pltpu.VMEM((n, 4, 128), f32),
            dma((planes,)),
            dma((4,)),
            dma((4,)),
            dma((n,)),
            dma((n,)),
            dma((n,)),
            dma((n,)),
        ],
        compiler_params=pltpu.CompilerParams(collective_id=0, has_side_effects=True),
    )(
        component_shares,
        thermal_ratio,
        fuel_share,
        species_mass_unit[None],
        formation_energy[None],
        frequency_factor[None],
        arrhenius_barrier[None],
        product_minus_reactant.T,
        particle_voxel_position[0],
        jnp.transpose(particle_voxel_offset[0], (1, 0, 2)),
        particle_active_total,
    )
    return samples[None]


def solution(mesh):
    placed = (
        P(None, ("snap", "gx"), None, None),
        P(("snap", "gx"), None, None),
        P(("snap", "gx"), None, None),
        P(),
        P(),
        P(),
        P(),
        P(),
        P(("snap", "gx"), None, None),
        P(("snap", "gx"), None, None, None),
        P(("snap", "gx"), None),
    )
    return jax.shard_map(
        local,
        mesh=mesh,
        in_specs=placed,
        out_specs=P(("snap", "gx"), None, None, None),
        check_vma=False,
    )
```

```python
import functools

import jax
import jax.numpy as jnp
from jax import lax
from jax.experimental import pallas as pl
from jax.experimental.pallas import tpu as pltpu
from jax.sharding import PartitionSpec as P

stencil_coeffs = (0.8, -0.2, 4.0 / 105.0, -1.0 / 280.0)
reach = 4
log2e = 1.4426950408889634
MESH = pl.DeviceIdType.MESH
f32 = jnp.float32
bf16 = jnp.bfloat16


def split3(x):
    hi = x.astype(bf16)
    rest = x - hi.astype(f32)
    mid = rest.astype(bf16)
    lo = (rest - mid.astype(f32)).astype(bf16)
    return hi, mid, lo


def split2(x):
    hi = x.astype(bf16)
    return hi, (x - hi.astype(f32)).astype(bf16)


def kernel(
    n,
    species_hbm,
    t_ref,
    fuel_ref,
    mass_ref,
    formation_ref,
    frequency_ref,
    barrier_ref,
    stoich_ref,
    pos_ref,
    off_ref,
    live_ref,
    out_ref,
    species,
    feat,
    weights,
    heat_weight,
    table,
    heat,
    fcat,
    halo_before,
    halo_after,
    edge_t,
    edge_out,
    edge_in,
    pack,
    recv,
    back,
    home,
    load_sem,
    halo_send,
    halo_recv,
    out_send,
    out_recv,
    home_send,
    home_recv,
):
    me = lax.axis_index("gx")
    nxt, prv = lax.rem(me + 1, n), lax.rem(me + n - 1, n)
    n_species, planes, ny, nz = species_hbm.shape
    slots = pos_ref.shape[1]
    reactions = stoich_ref.shape[1]
    padded = weights.shape[0]
    group = 32

    loads = [
        pltpu.make_async_copy(species_hbm.at[:, p], species.at[p], load_sem.at[p])
        for p in range(planes)
    ]
    for copy in loads:
        copy.start()

    barrier = pltpu.get_barrier_semaphore()

    def greet(k, _):
        pl.semaphore_signal(
            barrier, inc=1, device_id={"gx": lax.rem(me + k, n)}, device_id_type=MESH
        )
        return 0

    lax.fori_loop(1, n, greet, 0)

    def pack_one(d, _):
        pack[d, 0:1, 0:slots] = pos_ref[pl.ds(d, 1), :].astype(f32)
        for i in range(3):
            pack[d, i + 1 : i + 2, 0:slots] = off_ref[i, pl.ds(d, 1), :]
        return 0

    lax.fori_loop(0, n, pack_one, 0)

    table[...] = jnp.zeros_like(table)
    stoich = stoich_ref[...].astype(f32)
    orders = jnp.maximum(-stoich, 0.0)
    same = lax.broadcasted_iota(jnp.int32, (n_species, n_species), 0) == lax.broadcasted_iota(
        jnp.int32, (n_species, n_species), 1
    )
    log_mass = jnp.sum(jnp.where(same, jnp.log(mass_ref[...]), 0.0), axis=1, keepdims=True)
    formation = jnp.sum(jnp.where(same, formation_ref[...], 0.0), axis=1, keepdims=True)
    net = -jnp.sum(stoich * formation, axis=0, keepdims=True)
    offset = jnp.log(frequency_ref[...]) - jnp.sum(orders * log_mass, axis=0, keepdims=True)
    extra = [
        part.astype(f32)
        for row in (barrier_ref[...] * (-log2e), offset * log2e)
        for part in split3(row)
    ]
    for j in range(3):
        table[j * group : j * group + n_species, 0:reactions] = orders
        for i, row in enumerate(extra):
            r = j * group + n_species + i
            table[r : r + 1, 0:reactions] = row
    table[3 * group : 3 * group + 1, 0:reactions] = net
    columns = jnp.transpose(table[...])[0:padded]
    weights[...] = columns.astype(bf16)
    heat_weight[...] = jnp.broadcast_to(columns[:, 3 * group : 3 * group + 1], (padded, 128))

    step = ny + 1

    def put_feat(j, value):
        feat[j * step : j * step + ny, :] = value

    ones = jnp.ones((ny, nz), f32)
    for j in range(3):
        put_feat(n_species + 3 + j, ones)
    for j in range(n_species + 6, group):
        put_feat(j, jnp.zeros((ny, nz), f32))

    batch = 32

    def heat_plane(p):
        loads[p].wait()
        temper = t_ref[p]
        log_t = jnp.log(temper)
        for s in range(n_species):
            put_feat(s, (jnp.log(species[p, s]) - log_t) * log2e)
        inverse = 1.0 / temper
        for j in range(3):
            put_feat(n_species + j, inverse)

        def rows(i, _):
            for b in range(0, batch, 2):
                r = i * batch + b
                f = jnp.concatenate(
                    [
                        feat[pl.ds(r, group, stride=step), :],
                        feat[pl.ds(r + 1, group, stride=step), :],
                    ],
                    axis=1,
                )
                x = jnp.dot(
                    weights[:, 0 : 3 * group],
                    jnp.concatenate(split3(f), axis=0),
                    preferred_element_type=f32,
                )
                rate = jnp.exp2(x)
                hw = heat_weight[...]
                for h in range(2):
                    term = rate[:, h * 128 : (h + 1) * 128] * hw
                    total = jnp.sum(term.reshape(padded // 8, 8, 128), axis=0)
                    heat[pl.ds(p * ny + r + h, 1), :] = jnp.sum(total, axis=0, keepdims=True)
            return 0

        lax.fori_loop(0, ny // batch, rows, 0)

    def put(p, f, value):
        hi, lo = split2(value)
        r = (p * 4 + f) * ny
        fcat[r : r + ny, 0:nz] = hi
        fcat[r : r + ny, nz : 2 * nz] = lo

    def plane_of(q):
        if q < 0:
            return halo_before[q + reach]
        if q >= planes:
            return halo_after[q - planes]
        return fuel_ref[q]

    def dissip(p):
        centre = plane_of(p)
        gx = jnp.zeros_like(centre)
        gy = jnp.zeros_like(centre)
        gz = jnp.zeros_like(centre)
        for k in range(1, reach + 1):
            c = stencil_coeffs[k - 1]
            gx = gx + c * (plane_of(p + k) - plane_of(p - k))
            gy = gy + c * (pltpu.roll(centre, ny - k, 0) - pltpu.roll(centre, k, 0))
            gz = gz + c * (pltpu.roll(centre, nz - k, 1) - pltpu.roll(centre, k, 1))
        return jnp.exp(0.7 * jnp.log(t_ref[p])) * (gx * gx + gy * gy + gz * gz)

    def remote(src, dst, send, got, to):
        return pltpu.make_async_remote_copy(
            src_ref=src,
            dst_ref=dst,
            send_sem=send,
            recv_sem=got,
            device_id={"gx": to},
            device_id_type=MESH,
        )

    heat_plane(0)

    pl.semaphore_wait(barrier, n - 1)
    up = remote(
        fuel_ref.at[pl.ds(planes - reach, reach)], halo_before, halo_send.at[0], halo_recv.at[0], nxt
    )
    down = remote(fuel_ref.at[pl.ds(0, reach)], halo_after, halo_send.at[1], halo_recv.at[1], prv)
    down_t = remote(t_ref.at[0], edge_t, halo_send.at[2], halo_recv.at[2], prv)
    down_e = remote(edge_out, edge_in, halo_send.at[3], halo_recv.at[3], prv)
    up.start()

    def send_out(k, _):
        d = lax.rem(me + k, n)
        remote(pack.at[d], recv.at[me], out_send.at[d], out_recv.at[me], d).start()
        return 0

    lax.fori_loop(1, n, send_out, 0)
    down.start()
    down_t.start()
    recv[me] = pack[me]

    heat_plane(1)
    up.wait_recv()
    first = dissip(0)
    edge_out[0] = first
    edge_out[1] = heat[0:ny, :]
    for p in range(2, planes):
        heat_plane(p)
        if p == 2:
            down_e.start()
    down.wait_recv()
    for p in range(planes):
        put(p, 0, t_ref[p])
        put(p, 1, fuel_ref[p])
        put(p, 2, first if p == 0 else dissip(p))
        put(p, 3, heat[p * ny : (p + 1) * ny, :])
    down_t.wait_recv()
    down_e.wait_recv()
    put(planes, 0, edge_t[...])
    put(planes, 1, halo_after[0])
    put(planes, 2, edge_in[0])
    put(planes, 3, edge_in[1])

    def got_one(k, _):
        d = lax.rem(me + k, n)
        remote(pack.at[d], recv.at[d], out_send.at[d], out_recv.at[d], d).wait()
        return 0

    lax.fori_loop(1, n, got_one, 0)

    low = lax.broadcasted_iota(jnp.int32, (4, 128), 1) < slots
    z_label = lax.broadcasted_iota(jnp.int32, (nz, 256), 0).astype(f32)
    y_label = lax.broadcasted_iota(jnp.int32, (ny, 256), 0).astype(f32)

    def sample(turn, _):
        g = lax.rem(me // 4 + 1 + turn, n // 4)
        halves = [
            jnp.where(low, recv[4 * g + 2 * h], pltpu.roll(recv[4 * g + 2 * h + 1], slots, 1))
            for h in range(2)
        ]
        t = jnp.concatenate(halves, axis=1)
        cell, fx, fy, fz = (t[i : i + 1] for i in range(4))
        cx = jnp.floor((cell + 0.5) * (1.0 / (ny * nz)))
        cell = cell - cx * (ny * nz)
        cy = jnp.floor((cell + 0.5) * (1.0 / nz))
        cz = cell - cy * nz
        cy1 = jnp.where(cy + 1.0 >= ny, 0.0, cy + 1.0)
        cz1 = jnp.where(cz + 1.0 >= nz, 0.0, cz + 1.0)
        wz = jnp.where(z_label == cz, 1.0 - fz, jnp.where(z_label == cz1, fz, 0.0))
        wy = jnp.where(y_label == cy, 1.0 - fy, jnp.where(y_label == cy1, fy, 0.0))
        wh, wl = split2(wz)
        both = jnp.concatenate([wh, wh], axis=0)
        acc = jnp.zeros((4, 8, 256), f32)
        for p in range(planes + 1):
            rows = slice(p * 4 * ny, (p + 1) * 4 * ny)
            a = jnp.dot(fcat[rows, :], both, preferred_element_type=f32)
            a = a + jnp.dot(fcat[rows, 0:nz], wl, preferred_element_type=f32)
            wx = jnp.where(cx == p, 1.0 - fx, jnp.where(cx == p - 1.0, fx, 0.0))
            a = a.reshape(4, ny // 8, 8, 256) * wy.reshape(ny // 8, 8, 256)[None]
            acc = acc + jnp.sum(a, axis=1) * wx.reshape(1, 1, 256)
        v = jnp.sum(acc, axis=1)
        for j in range(4):
            s = 4 * g + j
            block = v[:, (j // 2) * 128 : (j // 2 + 1) * 128]
            if j % 2:
                block = pltpu.roll(block, 128 - slots, 1)
            back[s] = block

            @pl.when(s != me)
            def _():
                remote(back.at[s], home.at[me], home_send.at[s], home_recv.at[me], s).start()

        return 0

    lax.fori_loop(0, n // 4, sample, 0)
    home[me] = back[me]

    def home_one(k, _):
        d = lax.rem(me + k, n)
        remote(back.at[d], home.at[d], home_send.at[d], home_recv.at[d], d).wait()
        return 0

    lax.fori_loop(1, n, home_one, 0)
    for copy in (up, down, down_t, down_e):
        copy.wait_send()

    slot = lax.broadcasted_iota(jnp.int32, (4, slots), 1)

    def finish(d, _):
        out_ref[d] = jnp.where(slot < live_ref[0, d], home[d, :, 0:slots], 0.0)
        return 0

    lax.fori_loop(0, n, finish, 0)


def local(
    component_shares,
    thermal_ratio,
    fuel_share,
    species_mass_unit,
    formation_energy,
    frequency_factor,
    arrhenius_barrier,
    product_minus_reactant,
    particle_voxel_position,
    particle_voxel_offset,
    particle_active_total,
):
    n = lax.axis_size("gx")
    n_species, planes, ny, nz = component_shares.shape
    reactions = frequency_factor.shape[0]
    slots = particle_voxel_position.shape[2]
    padded = (reactions + 7) // 8 * 8
    vmem = pl.BlockSpec(memory_space=pltpu.VMEM)
    dma = pltpu.SemaphoreType.DMA
    samples = pl.pallas_call(
        functools.partial(kernel, n),
        out_shape=jax.ShapeDtypeStruct((n, 4, slots), f32),
        in_specs=[pl.BlockSpec(memory_space=pl.ANY)] + [vmem] * 9
        + [pl.BlockSpec(memory_space=pltpu.SMEM)],
        out_specs=vmem,
        scratch_shapes=[
            pltpu.VMEM((planes, n_species, ny, nz), f32),
            pltpu.VMEM((32 * (ny + 1), nz), f32),
            pltpu.VMEM((padded, 128), bf16),
            pltpu.VMEM((padded, 128), f32),
            pltpu.VMEM((128, (padded + 127) // 128 * 128), f32),
            pltpu.VMEM((planes * ny, nz), f32),
            pltpu.VMEM(((planes + 1) * 4 * ny, 2 * nz), bf16),
            pltpu.VMEM((reach, ny, nz), f32),
            pltpu.VMEM((reach, ny, nz), f32),
            pltpu.VMEM((ny, nz), f32),
            pltpu.VMEM((2, ny, nz), f32),
            pltpu.VMEM((2, ny, nz), f32),
            pltpu.VMEM((n, 4, 128), f32),
            pltpu.VMEM((n, 4, 128), f32),
            pltpu.VMEM((n, 4, 128), f32),
            pltpu.VMEM((n, 4, 128), f32),
            dma((planes,)),
            dma((4,)),
            dma((4,)),
            dma((n,)),
            dma((n,)),
            dma((n,)),
            dma((n,)),
        ],
        compiler_params=pltpu.CompilerParams(collective_id=0, has_side_effects=True),
    )(
        component_shares,
        thermal_ratio,
        fuel_share,
        species_mass_unit[None],
        formation_energy[None],
        frequency_factor[None],
        arrhenius_barrier[None],
        product_minus_reactant.T,
        particle_voxel_position[0],
        jnp.transpose(particle_voxel_offset[0], (1, 0, 2)),
        particle_active_total,
    )
    return samples[None]


def solution(mesh):
    placed = (
        P(None, ("snap", "gx"), None, None),
        P(("snap", "gx"), None, None),
        P(("snap", "gx"), None, None),
        P(),
        P(),
        P(),
        P(),
        P(),
        P(("snap", "gx"), None, None),
        P(("snap", "gx"), None, None, None),
        P(("snap", "gx"), None),
    )
    return jax.shard_map(
        local,
        mesh=mesh,
        in_specs=placed,
        out_specs=P(("snap", "gx"), None, None, None),
        check_vma=False,
    )
```
